256 devices in a mesh: dp: 16 (over z, core), mp: 16 (over y, x).
Axes of the slice: x: 4, y: 4, z: 8, core: 2. Of those that a mesh axis runs over, the one named last changes fastest.
Arguments:
- activations: bfloat16 [16, 1024, 4096], P('dp'), may hold values from -6 to 6
- out_grads: bfloat16 [16, 1024, 8192], P('dp', None, 'mp'), may hold values from -0.1875 to 0.1875
- error_fb: bfloat16 [16, 4096, 8192], P('dp', None, 'mp'), may hold values from -6 to 6
- q_prev: float32 [8192, 128], P('mp'), may hold values from -0.0625 to 0.0625
Outputs:
- new_error: bfloat16 [16, 4096, 8192], P('dp', None, 'mp')
- q_new: float32 [8192, 128], P('mp')
The draws below stay inside these ranges and needn't reach their ends.
All inputs are finite; a program needn't handle non-finite values.
Results may differ from the reference program's by a relative error of at most 0.001.
Values sent between devices are 32-bit elements; how exact they have to be, the bound alone decides.
A program may use at most 128 MiB of HBM per device.

```python
import jax
import jax.numpy as jnp
from jax import lax

D = 8192
ROWS = 4096
RANK = 128
TOK_DEV = 1024
REPLICAS = 16


def block_scale(rng, dims, shards, smallest, top_value):
    level, own = 1.0, jax.random.fold_in(rng, 6)
    for position, parts in shards:
        draws = jnp.exp(jax.random.uniform(jax.random.fold_in(own, position), (parts,), jnp.float32, smallest / len(shards), top_value / len(shards)))
        level = level * jnp.repeat(draws, dims[position] // parts).reshape([-1 if axis == position else 1 for axis in range(len(dims))])
    return level


def centred(own_key, shape, width, bound, shards=(), held_as=jnp.bfloat16):
    entries = width * jax.random.normal(own_key, shape, jnp.float32)
    if shards:
        entries = entries * block_scale(own_key, shape, shards, -0.22, 0.18)
    return jnp.clip(entries, -bound, bound).astype(held_as)


def setup_inputs(seed: int = 0) -> dict:
    splits = jax.random.split(jax.random.key(seed), 5)
    return {
        "activations": centred(splits[0], (REPLICAS, TOK_DEV, ROWS), 1.0, 6.0, ((0, 16),)),
        "out_grads": centred(splits[1], (REPLICAS, TOK_DEV, D), TOK_DEV ** -0.5, 0.1875, ((0, 16), (2, 16))),
        "error_fb": centred(splits[2], (REPLICAS, ROWS, D), 1.0, 6.0, ((0, 16), (2, 16))),
        "q_prev": centred(splits[3], (D, RANK), D ** -0.5, 0.0625, ((0, 16),), jnp.float32),
    }


def merge_one(act_r, grad_r, err_r):
    grad_full = lax.dot_general(act_r.astype(jnp.float32), grad_r.astype(jnp.float32), (((0,), (0,)), ((), ())), preferred_element_type=jnp.float32)
    return grad_full + err_r.astype(jnp.float32)

def reference(activations, out_grads, error_fb, q_prev):

    def step_fn(carry, items):
        merged = merge_one(items[0], items[1], items[2])
        term = jnp.dot(merged, q_prev, precision=lax.Precision.HIGHEST)
        return (carry + term, merged)
    p_init = jnp.zeros((ROWS, RANK), jnp.float32)
    p_sum, merged_all = lax.scan(step_fn, p_init, (activations, out_grads, error_fb))
    gram = jnp.dot(p_sum.T, p_sum, precision=lax.Precision.HIGHEST)
    chol = jnp.linalg.cholesky(gram)
    p_hat = lax.linalg.triangular_solve(chol, p_sum, left_side=False, lower=True, transpose_a=True)

    def q_fn(carry, merged):
        term = lax.dot_general(merged, p_hat, (((0,), (0,)), ((), ())), precision=lax.Precision.HIGHEST)
        return (carry + term, None)
    q_sum, unused = lax.scan(q_fn, jnp.zeros((D, RANK), jnp.float32), merged_all)
    q_new = q_sum / REPLICAS
    approx = jnp.dot(p_hat, q_new.T, precision=lax.Precision.HIGHEST)
    new_error = (merged_all - approx[None]).astype(jnp.bfloat16)
    return (new_error, q_new)
```

```python
import jax
import jax.numpy as jnp
from jax import lax
from jax.experimental import pallas as pl
from jax.experimental.pallas import tpu as pltpu
from jax.sharding import PartitionSpec as P

MESH = pl.DeviceIdType.MESH
NX, NY, NZ = 4, 4, 8


def position():
    dp, mp = lax.axis_index("dp"), lax.axis_index("mp")
    return lax.rem(mp, NX), mp // NX, dp // 2, lax.rem(dp, 2)


def device(x, y, z, c):
    return (z * 2 + c, y * NX + x)


def remote(src, dst, send, recv, where):
    return pltpu.make_async_remote_copy(
        src_ref=src, dst_ref=dst, send_sem=send, recv_sem=recv, device_id=where, device_id_type=MESH
    )


def drain(like, sem):
    pltpu.make_async_copy(like, like, sem).wait()


def loop(count, body):
    def step(k, carry):
        body(k)
        return carry

    lax.fori_loop(0, count, step, 0)


def sum_p_kernel(p, out, h, r0, r1, u, r2, v, r3, send, got0, got1, got2, got3, bak3, bak2, bak1, bak0):
    x, y, z, c = position()
    partner = device(x, y, z, 1 - c)
    turn = lambda own, d, n: lax.rem(own + d, n)
    xs = [device(turn(x, d, NX), y, z, c) for d in range(1, NX)]
    ys = [device(x, turn(y, d, NY), z, c) for d in range(1, NY)]
    zs = [device(x, y, turn(z, d, NZ), c) for d in range(1, NZ)]
    barrier = pltpu.get_barrier_semaphore()
    for peer in [partner] + xs + ys + zs:
        pl.semaphore_signal(barrier, inc=1, device_id=peer, device_id_type=MESH)
    pl.semaphore_wait(barrier, 1 + len(xs) + len(ys) + len(zs))

    def pair_out(k):
        remote(p.at[k, 1 - c], r0.at[k], send.at[0], got0.at[k], partner).start()

    loop(NZ, pair_out)

    def first(k):
        drain(r0.at[k], got0.at[k])
        h[k] = p[k, c] + r0[k]
        for d in range(1, NX):
            remote(h.at[k, 0, turn(x, d, NX)], r1.at[k, 0, d - 1], send.at[1], got1.at[k], xs[d - 1]).start()
            remote(h.at[k, 1, turn(y, d, NY)], r1.at[k, 1, d - 1], send.at[1], got1.at[k], ys[d - 1]).start()

    loop(NZ, first)

    def second(k):
        drain(r1.at[k], got1.at[k])
        for part, own in ((0, x), (1, y)):
            u[k, part] = h[k, part, own] + r1[k, part, 0] + r1[k, part, 1] + r1[k, part, 2]
        for d in range(1, NX):
            remote(u.at[k, 0, turn(y, d, NY)], r2.at[k, 0, d - 1], send.at[2], got2.at[k], ys[d - 1]).start()
            remote(u.at[k, 1, turn(x, d, NX)], r2.at[k, 1, d - 1], send.at[2], got2.at[k], xs[d - 1]).start()

    loop(NZ, second)

    def third(k):
        drain(r2.at[k], got2.at[k])
        for part, own in ((0, y), (1, x)):
            v[k, part] = u[k, part, own] + r2[k, part, 0] + r2[k, part, 1] + r2[k, part, 2]

        @pl.when(k != z)
        def _():
            remote(v.at[k], r3.at[lax.rem(z - k + NZ, NZ) - 1], send.at[3], got3, device(x, y, k, c)).start()

    loop(NZ, third)
    drain(r3, got3)
    total = v[z]
    for d in range(NZ - 1):
        total = total + r3[d]
    out[z, c, 0, x, y] = total[0]
    out[z, c, 1, y, x] = total[1]
    for d in range(1, NZ):
        for piece in (out.at[z, c, 0, x, y], out.at[z, c, 1, y, x]):
            remote(piece, piece, send.at[4], bak3.at[z], zs[d - 1]).start()

    def third_back(i):
        k = lax.rem(z + i, NZ)

        @pl.when(i != 0)
        def _():
            drain(v.at[k], bak3.at[k])

        for d in range(1, NX):
            a, b = out.at[k, c, 0, x, y], out.at[k, c, 1, y, x]
            remote(a, a, send.at[5], bak2.at[k], ys[d - 1]).start()
            remote(b, b, send.at[5], bak2.at[k], xs[d - 1]).start()

    loop(NZ, third_back)

    def second_back(i):
        k = lax.rem(z + i, NZ)
        drain(r2.at[k], bak2.at[k])
        for d in range(1, NX):
            a, b = out.at[k, c, 0, x], out.at[k, c, 1, y]
            remote(a, a, send.at[6], bak1.at[k], xs[d - 1]).start()
            remote(b, b, send.at[6], bak1.at[k], ys[d - 1]).start()

    loop(NZ, second_back)

    def first_back(i):
        k = lax.rem(z + i, NZ)
        drain(r1.at[k], bak1.at[k])
        remote(out.at[k, c], out.at[k, c], send.at[7], bak0.at[k], partner).start()

    loop(NZ, first_back)

    def pair_back(k):
        drain(r0.at[k], bak0.at[k])

    loop(NZ, pair_back)
    drain(r0, send.at[0])
    drain(r1, send.at[1])
    drain(r2, send.at[2])
    drain(r3, send.at[3])
    drain(r3, send.at[4])
    drain(r2, send.at[5])
    drain(r1, send.at[6])
    drain(r0, send.at[7])


def sum_p(p):
    shape = (NZ, 2, 2, NX, NY, 8, 128)
    f32 = lambda *dims: pltpu.VMEM(dims + (8, 128), jnp.float32)
    sem = pltpu.SemaphoreType.DMA
    out = pl.pallas_call(
        sum_p_kernel,
        out_shape=jax.ShapeDtypeStruct(shape, jnp.float32),
        in_specs=[pl.BlockSpec(memory_space=pltpu.VMEM)],
        out_specs=pl.BlockSpec(memory_space=pltpu.VMEM),
        scratch_shapes=[
            f32(NZ, 2, NX, NY),
            f32(NZ, 2, NX, NY),
            f32(NZ, 2, NX - 1, NY),
            f32(NZ, 2, NY),
            f32(NZ, 2, NY - 1),
            f32(NZ, 2),
            f32(NZ - 1, 2),
            sem((8,)),
            sem((NZ,)),
            sem((NZ,)),
            sem((NZ,)),
            sem(()),
            sem((NZ,)),
            sem((NZ,)),
            sem((NZ,)),
            sem((NZ,)),
        ],
        compiler_params=pltpu.CompilerParams(collective_id=0, has_side_effects=True),
    )(p.reshape(shape))
    return out.reshape(4096, 128)


def sum_s_kernel(s, out, h, r0, r1, w, send, got0, got1, bak1, bak0):
    x, y, z, c = position()
    partner = device(x, y, z, 1 - c)
    zs = [device(x, y, lax.rem(z + d, NZ), c) for d in range(1, NZ)]
    barrier = pltpu.get_barrier_semaphore()
    for peer in [partner] + zs:
        pl.semaphore_signal(barrier, inc=1, device_id=peer, device_id_type=MESH)
    pl.semaphore_wait(barrier, 1 + len(zs))
    remote(s.at[1 - c], r0, send.at[0], got0, partner).start()
    drain(r0, got0)
    h[...] = s[c] + r0[...]
    for d in range(1, NZ):
        remote(h.at[lax.rem(z + d, NZ)], r1.at[d - 1], send.at[1], got1, zs[d - 1]).start()
    drain(r1, got1)
    total = h[z]
    for d in range(NZ - 1):
        total = total + r1[d]
    w[...] = total
    out[c, z] = total
    for d in range(1, NZ):
        remote(w, out.at[c, z], send.at[2], bak1.at[z], zs[d - 1]).start()
    remote(w, out.at[c, z], send.at[3], bak0.at[z], partner).start()
    for d in range(1, NZ):
        k = lax.rem(z + d, NZ)
        drain(w, bak1.at[k])
        remote(out.at[c, k], out.at[c, k], send.at[3], bak0.at[k], partner).start()
    for k in range(NZ):
        drain(w, bak0.at[k])
    drain(r0, send.at[0])
    drain(r1, send.at[1])
    drain(r1, send.at[2])
    drain(r0, send.at[3])


def sum_s(s):
    shape = (2, NZ, 8, 512)
    f32 = lambda *dims: pltpu.VMEM(dims + (8, 512), jnp.float32)
    sem = pltpu.SemaphoreType.DMA
    out = pl.pallas_call(
        sum_s_kernel,
        out_shape=jax.ShapeDtypeStruct(shape, jnp.float32),
        in_specs=[pl.BlockSpec(memory_space=pltpu.VMEM)],
        out_specs=pl.BlockSpec(memory_space=pltpu.VMEM),
        scratch_shapes=[f32(NZ), f32(NZ), f32(NZ - 1), f32(), sem((4,)), sem(()), sem(()), sem((NZ,)), sem((NZ,))],
        compiler_params=pltpu.CompilerParams(collective_id=1, has_side_effects=True),
    )(s.reshape(shape))
    return out.reshape(128, 512)


def orthonormal(p_part, gram):
    chol = jnp.linalg.cholesky(gram)
    return lax.linalg.triangular_solve(chol, p_part, left_side=False, lower=True, transpose_a=True)


def self_gram(p_part):
    return jnp.dot(p_part.T, p_part, precision=lax.Precision.HIGHEST)


def per_device(activations, out_grads, error_fb, q_prev):
    grad_full = lax.dot_general(
        activations[0], out_grads[0], (((0,), (0,)), ((), ())), preferred_element_type=jnp.float32
    )
    merged = grad_full + error_fb[0].astype(jnp.float32)
    p_local = jnp.dot(merged, q_prev, precision=lax.Precision.HIGHEST)
    p_sum = sum_p(p_local)
    p_hat = orthonormal(p_sum, self_gram(p_sum))
    q_local_t = lax.dot_general(
        p_hat, merged, (((0,), (0,)), ((), ())), precision=lax.Precision.HIGHEST
    )
    q_new_t = sum_s(q_local_t) / lax.axis_size("dp")
    approx = jnp.dot(p_hat, q_new_t, precision=lax.Precision.HIGHEST)
    new_error = (merged - approx).astype(jnp.bfloat16)[None]
    return (new_error, q_new_t.T)


def solution(mesh):
    placed = (P("dp", None, None), P("dp", None, "mp"), P("dp", None, "mp"), P("mp", None))
    return jax.shard_map(
        per_device,
        mesh=mesh,
        in_specs=placed,
        out_specs=(P("dp", None, "mp"), P("mp", None)),
        check_vma=False,
    )
```

```python
import jax
import jax.numpy as jnp
from jax import lax
from jax.experimental import pallas as pl
from jax.experimental.pallas import tpu as pltpu
from jax.sharding import PartitionSpec as P

MESH = pl.DeviceIdType.MESH
NX, NY, NZ = 4, 4, 8
TOK, ROWS, COLS, RANK = 1024, 4096, 512, 128
CHUNK = ROWS // NZ
BLOCK = 16
BF, F32 = jnp.bfloat16, jnp.float32
HIGHEST = lax.Precision.HIGHEST
FIRST = (((0,), (0,)), ((), ()))


def position():
    dp, mp = lax.axis_index("dp"), lax.axis_index("mp")
    return lax.rem(mp, NX), mp // NX, dp // 2, lax.rem(dp, 2)


def device(x, y, z, c):
    return (z * 2 + c, y * NX + x)


def turn(own, d, n):
    return lax.rem(own + d, n)


def remote(src, dst, send, recv, where):
    return pltpu.make_async_remote_copy(
        src_ref=src, dst_ref=dst, send_sem=send, recv_sem=recv, device_id=where, device_id_type=MESH
    )


def drain(like, sem):
    pltpu.make_async_copy(like, like, sem).wait()


def loop(first, last, body):
    def step(k, carry):
        body(k)
        return carry

    lax.fori_loop(first, last, step, 0)


def halves(value):
    high = value.astype(BF)
    return high, (value - high.astype(F32)).astype(BF)


def dot(a, b, dims=(((1,), (0,)), ((), ()))):
    return lax.dot_general(a, b, dims, preferred_element_type=F32)


def eliminate(m, b):
    at = b * BLOCK
    block = m[at : at + BLOCK, :]
    row = lax.broadcasted_iota(jnp.int32, (BLOCK, 1), 0)
    for j in range(BLOCK):
        scale = lax.rsqrt(block[j : j + 1, at + j : at + j + 1])
        pivot = block[j : j + 1, :] * scale
        factor = block[:, at + j : at + j + 1] * scale
        block = jnp.where(row == j, pivot, jnp.where(row > j, block - factor * pivot, block))
    m[at : at + BLOCK, :] = block
    if at + BLOCK < RANK:
        update = lax.dot_general(block[:, :RANK], block, FIRST, precision=HIGHEST, preferred_element_type=F32)
        m[at + BLOCK :, :] -= update[at + BLOCK :, :]


def step_kernel(
    a, g, e, q,
    hi_out, lo_out, p_out, w_out, q_out,
    abuf, ebuf, gbuf, hi, lo, qcat, p, h, r0, r1, u, r2, v, r3, full, both,
    acc, sq, cross, m, s, s0, hs, s1, sw, sall,
    asem, esem, gsem, osem, send, got0, got1, got2, got3, bak3, bak2, bak1, bak0,
    ssend, sgot0, sgot1, sbak1, sbak0,
):
    x, y, z, c = position()
    partner = device(x, y, z, 1 - c)
    xs = [device(turn(x, d, NX), y, z, c) for d in range(1, NX)]
    ys = [device(x, turn(y, d, NY), z, c) for d in range(1, NY)]
    zs = [device(x, y, turn(z, d, NZ), c) for d in range(1, NZ)]
    rows = lambda k: pl.ds(pl.multiple_of(k * CHUNK, CHUNK), CHUNK)

    def loads(k, slot):
        return (
            pltpu.make_async_copy(a.at[:, rows(k)], abuf.at[slot], asem.at[slot]),
            pltpu.make_async_copy(e.at[rows(k)], ebuf.at[slot], esem.at[slot]),
        )

    whole_g = pltpu.make_async_copy(g, gbuf, gsem)
    whole_g.start()
    for copy in loads(0, 0):
        copy.start()
    barrier = pltpu.get_barrier_semaphore()
    for peer in [partner] + xs + ys + zs:
        pl.semaphore_signal(barrier, inc=1, device_id=peer, device_id_type=MESH)
    q_high, q_low = halves(q[...])
    qcat[:, :RANK] = q_high
    qcat[:, RANK:] = q_low
    acc[...] = jnp.zeros_like(acc)
    sq[...] = jnp.zeros_like(sq)
    cross[...] = jnp.zeros_like(cross)
    whole_g.wait()

    def compute(k):
        slot = lax.rem(k, 2)

        @pl.when(k < NZ - 1)
        def _():
            for copy in loads(k + 1, 1 - slot):
                copy.start()

        for copy in loads(k, slot):
            copy.wait()
        merged = dot(abuf[slot], gbuf[...], FIRST) + ebuf[slot].astype(F32)
        high, low = halves(merged)
        hi[rows(k)] = high
        lo[rows(k)] = low
        wide = dot(high, qcat[...])
        part = wide[:, :RANK] + wide[:, RANK:] + dot(low, qcat[:, :RANK])
        p[k] = part.reshape(2, 2, NX, NY, 8, RANK)
        pltpu.make_async_copy(hi.at[rows(k)], hi_out.at[rows(k)], osem.at[0]).start()
        pltpu.make_async_copy(lo.at[rows(k)], lo_out.at[rows(k)], osem.at[1]).start()

    def pair(k):
        remote(p.at[k, 1 - c], r0.at[k], send.at[0], got0.at[k], partner).start()

    def first(k):
        drain(r0.at[k], got0.at[k])
        h[k] = p[k, c] + r0[k]
        for d in range(1, NX):
            remote(h.at[k, 0, turn(x, d, NX)], r1.at[k, 0, d - 1], send.at[1], got1.at[k], xs[d - 1]).start()
            remote(h.at[k, 1, turn(y, d, NY)], r1.at[k, 1, d - 1], send.at[1], got1.at[k], ys[d - 1]).start()

    def second(k):
        drain(r1.at[k], got1.at[k])
        for part, own in ((0, x), (1, y)):
            u[k, part] = h[k, part, own] + r1[k, part, 0] + r1[k, part, 1] + r1[k, part, 2]
        for d in range(1, NX):
            remote(u.at[k, 0, turn(y, d, NY)], r2.at[k, 0, d - 1], send.at[2], got2.at[k], ys[d - 1]).start()
            remote(u.at[k, 1, turn(x, d, NX)], r2.at[k, 1, d - 1], send.at[2], got2.at[k], xs[d - 1]).start()

    def third(k):
        drain(r2.at[k], got2.at[k])
        for part, own in ((0, y), (1, x)):
            v[k, part] = u[k, part, own] + r2[k, part, 0] + r2[k, part, 1] + r2[k, part, 2]

        @pl.when(k != z)
        def _():
            remote(v.at[k], r3.at[lax.rem(z - k + NZ, NZ) - 1], send.at[3], got3, device(x, y, k, c)).start()

    pl.semaphore_wait(barrier, 1 + len(xs) + len(ys) + len(zs))
    lag1, lag2, lag3 = 1, 4, 6

    def forward(k):
        compute(k)
        pair(k)

        @pl.when(k >= lag1)
        def _():
            first(k - lag1)

        @pl.when(k >= lag2)
        def _():
            second(k - lag2)

        @pl.when(k >= lag3)
        def _():
            third(k - lag3)

    loop(0, NZ, forward)
    loop(NZ - lag1, NZ, first)
    loop(NZ - lag2, NZ, second)
    loop(NZ - lag3, NZ, third)
    drain(r3, got3)
    total = v[z]
    for d in range(NZ - 1):
        total = total + r3[d]
    full[z, c, 0, x, y] = total[0]
    full[z, c, 1, y, x] = total[1]
    for d in range(1, NZ):
        for piece in (full.at[z, c, 0, x, y], full.at[z, c, 1, y, x]):
            remote(piece, piece, send.at[4], bak3.at[z], zs[d - 1]).start()

    def third_back(i):
        k = turn(z, i, NZ)

        @pl.when(i != 0)
        def _():
            drain(v.at[k], bak3.at[k])

        for d in range(1, NX):
            one, two = full.at[k, c, 0, x, y], full.at[k, c, 1, y, x]
            remote(one, one, send.at[5], bak2.at[k], ys[d - 1]).start()
            remote(two, two, send.at[5], bak2.at[k], xs[d - 1]).start()

    def second_back(i):
        k = turn(z, i, NZ)
        drain(r2.at[k], bak2.at[k])
        for d in range(1, NX):
            one, two = full.at[k, c, 0, x], full.at[k, c, 1, y]
            remote(one, one, send.at[6], bak1.at[k], xs[d - 1]).start()
            remote(two, two, send.at[6], bak1.at[k], ys[d - 1]).start()

    def first_back(i):
        k = turn(z, i, NZ)
        drain(r1.at[k], bak1.at[k])
        remote(full.at[k, c], full.at[k, c], send.at[7], bak0.at[k], partner).start()

    def use(i):
        k = turn(z, i, NZ)
        drain(r0.at[k], bak0.at[k])
        block = full[k].reshape(CHUNK, RANK)
        high, low = halves(block)
        rest = ((block - high.astype(F32)) - low.astype(F32)).astype(BF)
        both[rows(k), :RANK] = high
        both[rows(k), RANK:] = low
        pltpu.make_async_copy(both.at[rows(k)], p_out.at[rows(k)], osem.at[2]).start()
        pair_ = both[rows(k)]
        acc[...] += dot(pair_, hi[rows(k)], FIRST)
        acc[:RANK] += dot(high, lo[rows(k)], FIRST)
        sq[...] += dot(pair_, pair_, FIRST)
        cross[...] += dot(high, rest, FIRST)

    loop(0, NZ, third_back)
    loop(0, NZ, second_back)

    def backward(i):
        first_back(i)

        @pl.when(i >= 1)
        def _():
            use(i - 1)

    loop(0, NZ, backward)
    use(NZ - 1)

    s[...] = (acc[:RANK] + acc[RANK:]).reshape(2, NZ, 8, COLS)
    remote(s.at[1 - c], s0, ssend.at[0], sgot0, partner).start()
    mixed = sq[:RANK, RANK:] + cross[...]
    m[:, :RANK] = sq[:RANK, :RANK] + (sq[RANK:, RANK:] + (mixed + mixed.T))
    diagonal = lax.broadcasted_iota(jnp.int32, (RANK, RANK), 0) == lax.broadcasted_iota(jnp.int32, (RANK, RANK), 1)
    m[:, RANK:] = diagonal.astype(F32)
    eliminate(m, 0)
    drain(s0, sgot0)
    hs[...] = s[c] + s0[...]
    for d in range(1, NZ):
        remote(hs.at[turn(z, d, NZ)], s1.at[d - 1], ssend.at[1], sgot1, zs[d - 1]).start()
    for b in (1, 2, 3, 4):
        eliminate(m, b)
    drain(s1, sgot1)
    total = hs[z]
    for d in range(NZ - 1):
        total = total + s1[d]
    sw[...] = total
    sall[c, z] = total
    for d in range(1, NZ):
        remote(sw, sall.at[c, z], ssend.at[2], sbak1.at[z], zs[d - 1]).start()
    remote(sw, sall.at[c, z], ssend.at[3], sbak0.at[z], partner).start()
    for b in (5, 6, 7):
        eliminate(m, b)

    def relay(i):
        k = turn(z, i, NZ)
        drain(sw, sbak1.at[k])
        remote(sall.at[c, k], sall.at[c, k], ssend.at[3], sbak0.at[k], partner).start()

    loop(1, NZ, relay)

    def arrive(k):
        drain(sw, sbak0.at[k])

    loop(0, NZ, arrive)
    inverse = m[:, RANK:]
    scaled = sall[...].reshape(RANK, COLS) * (1.0 / (2 * NZ))
    q_new = jnp.dot(inverse, scaled, precision=HIGHEST, preferred_element_type=F32)
    q_out[...] = q_new
    w_out[...] = lax.dot_general(inverse, q_new, FIRST, precision=HIGHEST, preferred_element_type=F32)

    drain(r0, send.at[0])
    drain(r1, send.at[1])
    drain(r2, send.at[2])
    drain(r3, send.at[3])
    drain(r3, send.at[4])
    drain(r2, send.at[5])
    drain(r1, send.at[6])
    drain(r0, send.at[7])
    drain(s0, ssend.at[0])
    drain(s1, ssend.at[1])
    drain(s1, ssend.at[2])
    drain(s0, ssend.at[3])
    pltpu.make_async_copy(hi, hi_out, osem.at[0]).wait()
    pltpu.make_async_copy(lo, lo_out, osem.at[1]).wait()
    pltpu.make_async_copy(both, p_out, osem.at[2]).wait()


def step(activations, out_grads, error_fb, q_prev):
    anywhere = pl.BlockSpec(memory_space=pl.ANY)
    near = pl.BlockSpec(memory_space=pltpu.VMEM)
    vm = lambda *dims: pltpu.VMEM(dims, F32)
    bf = lambda *dims: pltpu.VMEM(dims, BF)
    sem = lambda *dims: pltpu.SemaphoreType.DMA(dims)
    return pl.pallas_call(
        step_kernel,
        out_shape=[
            jax.ShapeDtypeStruct((ROWS, COLS), BF),
            jax.ShapeDtypeStruct((ROWS, COLS), BF),
            jax.ShapeDtypeStruct((ROWS, 2 * RANK), BF),
            jax.ShapeDtypeStruct((RANK, COLS), F32),
            jax.ShapeDtypeStruct((RANK, COLS), F32),
        ],
        in_specs=[anywhere, anywhere, anywhere, near],
        out_specs=[anywhere, anywhere, anywhere, near, near],
        scratch_shapes=[
            bf(2, TOK, CHUNK),
            bf(2, CHUNK, COLS),
            bf(TOK, COLS),
            bf(ROWS, COLS),
            bf(ROWS, COLS),
            bf(COLS, 2 * RANK),
            vm(NZ, 2, 2, NX, NY, 8, RANK),
            vm(NZ, 2, NX, NY, 8, RANK),
            vm(NZ, 2, NX, NY, 8, RANK),
            vm(NZ, 2, NX - 1, NY, 8, RANK),
            vm(NZ, 2, NY, 8, RANK),
            vm(NZ, 2, NY - 1, 8, RANK),
            vm(NZ, 2, 8, RANK),
            vm(NZ - 1, 2, 8, RANK),
            vm(NZ, 2, 2, NX, NY, 8, RANK),
            bf(ROWS, 2 * RANK),
            vm(2 * RANK, COLS),
            vm(2 * RANK, 2 * RANK),
            vm(RANK, RANK),
            vm(RANK, 2 * RANK),
            vm(2, NZ, 8, COLS),
            vm(NZ, 8, COLS),
            vm(NZ, 8, COLS),
            vm(NZ - 1, 8, COLS),
            vm(8, COLS),
            vm(2, NZ, 8, COLS),
            sem(2),
            sem(2),
            sem(),
            sem(3),
            sem(8),
            sem(NZ),
            sem(NZ),
            sem(NZ),
            sem(),
            sem(NZ),
            sem(NZ),
            sem(NZ),
            sem(NZ),
            sem(4),
            sem(),
            sem(),
            sem(NZ),
            sem(NZ),
        ],
        compiler_params=pltpu.CompilerParams(
            collective_id=0, has_side_effects=True, vmem_limit_bytes=40 << 20
        ),
        name="step",
    )(activations, out_grads, error_fb, q_prev)


def finish_kernel(p, w, q_t, hi, lo, out, q_new):
    @pl.when(pl.program_id(0) == 0)
    def _():
        q_new[...] = q_t[...].T

    high, low = halves(w[...])
    approx = dot(p[...], jnp.concatenate([high, high], axis=0)) + dot(p[:, :RANK], low)
    out[...] = ((hi[...].astype(F32) - approx) + lo[...].astype(F32)).astype(BF)


def finish(p, w, q_t, hi, lo):
    tile = 1024
    fixed = lambda *dims: pl.BlockSpec(dims, lambda i: (0, 0))
    moving = lambda *dims: pl.BlockSpec(dims, lambda i: (i, 0))
    return pl.pallas_call(
        finish_kernel,
        out_shape=[jax.ShapeDtypeStruct((ROWS, COLS), BF), jax.ShapeDtypeStruct((COLS, RANK), F32)],
        grid=(ROWS // tile,),
        in_specs=[
            moving(tile, 2 * RANK), fixed(RANK, COLS), fixed(RANK, COLS), moving(tile, COLS), moving(tile, COLS)
        ],
        out_specs=[moving(tile, COLS), fixed(COLS, RANK)],
        compiler_params=pltpu.CompilerParams(vmem_limit_bytes=24 << 20),
        name="finish",
    )(p, w, q_t, hi, lo)


def per_device(activations, out_grads, error_fb, q_prev):
    hi, lo, p, w, q_t = step(activations[0], out_grads[0], error_fb[0], q_prev)
    new_error, q_new = finish(p, w, q_t, hi, lo)
    return (new_error[None], q_new)


def solution(mesh):
    placed = (P("dp", None, None), P("dp", None, "mp"), P("dp", None, "mp"), P("mp", None))
    return jax.shard_map(
        per_device,
        mesh=mesh,
        in_specs=placed,
        out_specs=(P("dp", None, "mp"), P("mp", None)),
        check_vma=False,
    )
```

```python
import jax
import jax.numpy as jnp
from jax import lax
from jax.experimental import pallas as pl
from jax.experimental.pallas import tpu as pltpu
from jax.sharding import PartitionSpec as P

MESH = pl.DeviceIdType.MESH
NX, NY, NZ = 4, 4, 8
TOK, ROWS, COLS, RANK = 1024, 4096, 512, 128
CHUNKS = 4
CHUNK = ROWS // CHUNKS
SUB = CHUNK // (4 * NX * NY)
MERGE = 512
BLOCK, GROUP = 32, 16
QUARTERS = COLS // RANK
BF, F32 = jnp.bfloat16, jnp.float32
HIGHEST = lax.Precision.HIGHEST
FIRST = (((0,), (0,)), ((), ()))


def position():
    dp, mp = lax.axis_index("dp"), lax.axis_index("mp")
    return lax.rem(mp, NX), mp // NX, dp // 2, lax.rem(dp, 2)


def device(x, y, z, c):
    return (z * 2 + c, y * NX + x)


def turn(own, d, n):
    return lax.rem(own + d, n)


def remote(src, dst, send, recv, where):
    return pltpu.make_async_remote_copy(
        src_ref=src, dst_ref=dst, send_sem=send, recv_sem=recv, device_id=where, device_id_type=MESH
    )


def drain(like, sem):
    pltpu.make_async_copy(like, like, sem).wait()


def loop(first, last, body):
    def step(k, carry):
        body(k)
        return carry

    lax.fori_loop(first, last, step, 0)


def halves(value):
    high = value.astype(BF)
    return high, (value - high.astype(F32)).astype(BF)


def dot(a, b, dims=(((1,), (0,)), ((), ()))):
    return lax.dot_general(a, b, dims, preferred_element_type=F32)


def eliminate(m, b):
    at = b * BLOCK
    row = lax.broadcasted_iota(jnp.int32, (BLOCK, RANK), 0)
    sides = [m[at : at + BLOCK, :RANK], m[at : at + BLOCK, RANK:]]
    for start in range(0, BLOCK, GROUP):
        columns = [
            jnp.broadcast_to(sides[0][:, at + j : at + j + 1], (BLOCK, RANK)) for j in range(start, start + GROUP)
        ]
        for t in range(GROUP):
            j = start + t
            scale = lax.rsqrt(columns[t][j : j + 1, :])
            factor = jnp.where(row > j, columns[t] * scale, 0.0)
            for other in range(t + 1, GROUP):
                columns[other] = columns[other] - factor * factor[start + other : start + other + 1, :]
            for i in range(2):
                pivot = sides[i][j : j + 1, :] * scale
                sides[i] = jnp.where(row == j, pivot, sides[i] - factor * pivot)
    block = jnp.concatenate(sides, axis=1)
    m[at : at + BLOCK, :] = block
    if at + BLOCK < RANK:
        update = lax.dot_general(sides[0], block, FIRST, precision=HIGHEST, preferred_element_type=F32)
        m[at + BLOCK :, :] -= update[at + BLOCK :, :]


def step_kernel(
    a, g, e, q,
    hi, lo, both, w_out, q_out,
    abuf, ebuf, gbuf, qbuf, tcat, qcat, p, h, r0, r1, u, r2, zs_buf, full,
    acc, sq, cross, m, s, s0, hs, s1, sall,
    asem, esem, gsem, qsem, send, got0, got1, got2, got3, got4, bak2, bak1, bak0,
    ssend, sgot0, sgot1, sbak1, sbak0,
):
    x, y, z, c = position()
    partner = device(x, y, z, 1 - c)
    xs = [device(turn(x, d, NX), y, z, c) for d in range(1, NX)]
    ys = [device(x, turn(y, d, NY), z, c) for d in range(1, NY)]
    zs = [device(x, y, turn(z, d, NZ), c) for d in range(1, NZ)]
    rows = lambda k: pl.ds(pl.multiple_of(k * CHUNK, CHUNK), CHUNK)

    barrier = pltpu.get_barrier_semaphore()
    for peer in zs + xs + ys + [partner]:
        pl.semaphore_signal(barrier, inc=1, device_id=peer, device_id_type=MESH)

    def load_a(k):
        return pltpu.make_async_copy(a.at[:, rows(k)], abuf.at[:, rows(k)], asem.at[k])

    def load_e(k):
        return pltpu.make_async_copy(e.at[rows(k)], ebuf.at[rows(k)], esem.at[k])

    load_q = pltpu.make_async_copy(q, qbuf, qsem)
    load_g = pltpu.make_async_copy(g, gbuf, gsem)
    load_q.start()
    load_g.start()

    def load(k):
        load_a(k).start()
        load_e(k).start()

    loop(0, CHUNKS, load)
    acc[...] = jnp.zeros_like(acc)
    sq[...] = jnp.zeros_like(sq)
    cross[...] = jnp.zeros_like(cross)
    load_q.wait()
    q_high, q_low = halves(qbuf[...])
    qcat[:, :RANK] = q_high
    qcat[:, RANK:] = q_low
    load_g.wait()
    wide = dot(gbuf[...], qcat[...])
    t_high, t_low = halves(wide[:, :RANK] + wide[:, RANK:])
    tcat[:, :RANK] = t_high
    tcat[:, RANK:] = t_low

    def left(k):
        load_a(k).wait()
        load_e(k).wait()
        wide = dot(abuf[:, rows(k)], tcat[...], FIRST) + dot(ebuf[rows(k)], qcat[...])
        p[k] = (wide[:, :RANK] + wide[:, RANK:]).reshape(2, 2, NX, NY, SUB, RANK)

    def merge(n):
        part = pl.ds(pl.multiple_of(n * MERGE, MERGE), MERGE)
        high, low = halves(dot(abuf[:, part], gbuf[...], FIRST) + ebuf[part].astype(F32))
        hi[part] = high
        lo[part] = low

    def pair(k):
        remote(p.at[k, 1 - c], r0.at[k], send.at[0], got0.at[k], partner).start()

    def first(k):
        drain(r0.at[k], got0.at[k])
        h[k] = p[k, c] + r0[k]
        for d in range(1, NX):
            remote(h.at[k, 0, turn(x, d, NX)], r1.at[k, 0, d - 1], send.at[1], got1.at[k], xs[d - 1]).start()
            remote(h.at[k, 1, turn(y, d, NY)], r1.at[k, 1, d - 1], send.at[1], got1.at[k], ys[d - 1]).start()

    def second(k):
        drain(r1.at[k], got1.at[k])
        for part, own in ((0, x), (1, y)):
            u[k, part] = h[k, part, own] + r1[k, part, 0] + r1[k, part, 1] + r1[k, part, 2]
        for d in range(1, NX):
            remote(u.at[k, 0, turn(y, d, NY)], r2.at[k, 0, d - 1], send.at[2], got2.at[k], ys[d - 1]).start()
            remote(u.at[k, 1, turn(x, d, NX)], r2.at[k, 1, d - 1], send.at[2], got2.at[k], xs[d - 1]).start()

    def third(k):
        drain(r2.at[k], got2.at[k])
        for part, own in ((0, y), (1, x)):
            zs_buf[k, z, part] = u[k, part, own] + r2[k, part, 0] + r2[k, part, 1] + r2[k, part, 2]
        for d in (1, 2, NZ - 2, NZ - 1):
            remote(zs_buf.at[k, z], zs_buf.at[k, z], send.at[3], got3.at[k], zs[d - 1]).start()

    def onward(k):
        drain(zs_buf.at[k, pl.ds(0, 4)], got3.at[k])
        for part, way in ((0, 1), (1, NZ - 1)):
            origin = turn(z, NZ - 2 if way == 1 else 2, NZ)
            whole, half = zs_buf.at[k, origin], zs_buf.at[k, origin, part]
            remote(whole, whole, send.at[7], got4.at[k], zs[way - 1]).start()
            remote(half, half, send.at[7], got4.at[k], zs[(2 * way) % NZ - 1]).start()

    def second_back(k):
        drain(zs_buf.at[k, pl.ds(0, 3)], got4.at[k])
        total = zs_buf[k, 0]
        for other in range(1, NZ):
            total = total + zs_buf[k, other]
        full[k, c, 0, x, y] = total[0]
        full[k, c, 1, y, x] = total[1]
        for d in range(1, NX):
            one, two = full.at[k, c, 0, x, y], full.at[k, c, 1, y, x]
            remote(one, one, send.at[4], bak2.at[k], ys[d - 1]).start()
            remote(two, two, send.at[4], bak2.at[k], xs[d - 1]).start()

    def first_back(k):
        drain(r2.at[k], bak2.at[k])
        for d in range(1, NX):
            one, two = full.at[k, c, 0, x], full.at[k, c, 1, y]
            remote(one, one, send.at[5], bak1.at[k], xs[d - 1]).start()
            remote(two, two, send.at[5], bak1.at[k], ys[d - 1]).start()

    def pair_back(k):
        drain(r1.at[k], bak1.at[k])
        remote(full.at[k, c], full.at[k, c], send.at[6], bak0.at[k], partner).start()

    def use(k):
        drain(r0.at[k], bak0.at[k])
        block = full[k].reshape(CHUNK, RANK)
        high, low = halves(block)
        rest = ((block - high.astype(F32)) - low.astype(F32)).astype(BF)
        both[rows(k), :RANK] = high
        both[rows(k), RANK:] = low
        wide = both[rows(k)]
        acc[...] += dot(wide, hi[rows(k)], FIRST)
        acc[:RANK] += dot(high, lo[rows(k)], FIRST)
        sq[...] += dot(wide, wide, FIRST)
        cross[...] += dot(high, rest, FIRST)

    early = 3
    loop(0, early, left)
    pl.semaphore_wait(barrier, 1 + len(xs) + len(ys) + len(zs))
    loop(0, early, pair)

    def late(k):
        left(k)
        pair(k)

    loop(early, CHUNKS, late)
    ahead = 3
    loop(0, ahead, first)
    stages = (
        (second, 3, 0, CHUNKS), (first, 0, ahead, CHUNKS), (third, 5, 0, CHUNKS), (onward, 8, 0, CHUNKS),
        (second_back, 10, 0, CHUNKS), (first_back, 12, 0, CHUNKS), (pair_back, 15, 0, CHUNKS),
        (merge, 0, 0, ROWS // MERGE), (use, 16, 0, CHUNKS),
    )

    def slot(t):
        for stage, lag, start, stop in stages:
            @pl.when((t >= lag + start) & (t < lag + stop))
            def _():
                stage(t - lag)

    loop(0, stages[-1][1] + CHUNKS, slot)

    own = acc[:RANK] + acc[RANK:]
    for n in range(QUARTERS):
        s[n] = own[:, n * RANK : (n + 1) * RANK].reshape(2, NZ, 8, RANK)
        remote(s.at[n, 1 - c], s0.at[n], ssend.at[0], sgot0.at[n], partner).start()
    mixed = sq[:RANK, RANK:] + cross[...]
    m[:, :RANK] = sq[:RANK, :RANK] + (sq[RANK:, RANK:] + (mixed + mixed.T))
    diagonal = lax.broadcasted_iota(jnp.int32, (RANK, RANK), 0) == lax.broadcasted_iota(jnp.int32, (RANK, RANK), 1)
    m[:, RANK:] = diagonal.astype(F32)

    def spread(n):
        drain(s0.at[n], sgot0.at[n])
        hs[n] = s[n, c] + s0[n]
        for d in range(1, NZ):
            remote(hs.at[n, turn(z, d, NZ)], s1.at[n, d - 1], ssend.at[1], sgot1.at[n], zs[d - 1]).start()

    def gather(n):
        drain(s1.at[n], sgot1.at[n])
        total = hs[n, z]
        for d in range(NZ - 1):
            total = total + s1[n, d]
        sall[n, c, z] = total
        piece = sall.at[n, c, z]
        for d in range(1, NZ):
            remote(piece, piece, ssend.at[2], sbak1.at[n], zs[d - 1]).start()

    def share(n):
        drain(s1.at[n], sbak1.at[n])
        remote(sall.at[n, c], sall.at[n, c], ssend.at[3], sbak0.at[n], partner).start()

    def factors(ns):
        for n in ns:
            drain(s0.at[n], sbak0.at[n])
        inverse = m[:, RANK:]
        scaled = jnp.concatenate([sall[n].reshape(RANK, RANK) for n in ns], axis=1) * (1.0 / (2 * NZ))
        q_new = jnp.dot(inverse, scaled, precision=HIGHEST, preferred_element_type=F32)
        columns = slice(ns[0] * RANK, (ns[-1] + 1) * RANK)
        q_out[:, columns] = q_new
        w_out[:, columns] = lax.dot_general(inverse, q_new, FIRST, precision=HIGHEST, preferred_element_type=F32)

    eliminate(m, 0)
    loop(0, QUARTERS, spread)
    eliminate(m, 1)
    eliminate(m, 2)
    eliminate(m, 3)
    loop(0, QUARTERS, gather)
    loop(0, QUARTERS, share)
    factors((0, 1))
    factors((2, 3))

    drain(r0, send.at[0])
    drain(r1, send.at[1])
    drain(r2, send.at[2])
    drain(zs_buf.at[:, pl.ds(0, 4)], send.at[3])
    drain(zs_buf.at[:, pl.ds(0, 3)], send.at[7])
    drain(r2, send.at[4])
    drain(r1, send.at[5])
    drain(r0, send.at[6])
    drain(s0, ssend.at[0])
    drain(s1, ssend.at[1])
    drain(s1, ssend.at[2])
    drain(s0, ssend.at[3])


def step(activations, out_grads, error_fb, q_prev):
    far = pl.BlockSpec(memory_space=pltpu.HBM)
    near = pl.BlockSpec(memory_space=pltpu.VMEM)
    vm = lambda *dims: pltpu.VMEM(dims, F32)
    bf = lambda *dims: pltpu.VMEM(dims, BF)
    sem = lambda *dims: pltpu.SemaphoreType.DMA(dims)
    return pl.pallas_call(
        step_kernel,
        out_shape=[
            jax.ShapeDtypeStruct((ROWS, COLS), BF),
            jax.ShapeDtypeStruct((ROWS, COLS), BF),
            jax.ShapeDtypeStruct((ROWS, 2 * RANK), BF),
            jax.ShapeDtypeStruct((RANK, COLS), F32),
            jax.ShapeDtypeStruct((RANK, COLS), F32),
        ],
        in_specs=[far] * 4,
        out_specs=[near] * 5,
        scratch_shapes=[
            bf(TOK, ROWS),
            bf(ROWS, COLS),
            bf(TOK, COLS),
            vm(COLS, RANK),
            bf(TOK, 2 * RANK),
            bf(COLS, 2 * RANK),
            vm(CHUNKS, 2, 2, NX, NY, SUB, RANK),
            vm(CHUNKS, 2, NX, NY, SUB, RANK),
            vm(CHUNKS, 2, NX, NY, SUB, RANK),
            vm(CHUNKS, 2, NX - 1, NY, SUB, RANK),
            vm(CHUNKS, 2, NY, SUB, RANK),
            vm(CHUNKS, 2, NY - 1, SUB, RANK),
            vm(CHUNKS, NZ, 2, SUB, RANK),
            vm(CHUNKS, 2, 2, NX, NY, SUB, RANK),
            vm(2 * RANK, COLS),
            vm(2 * RANK, 2 * RANK),
            vm(RANK, RANK),
            vm(RANK, 2 * RANK),
            vm(QUARTERS, 2, NZ, 8, RANK),
            vm(QUARTERS, NZ, 8, RANK),
            vm(QUARTERS, NZ, 8, RANK),
            vm(QUARTERS, NZ - 1, 8, RANK),
            vm(QUARTERS, 2, NZ, 8, RANK),
            sem(CHUNKS),
            sem(CHUNKS),
            sem(),
            sem(),
            sem(8),
            sem(CHUNKS),
            sem(CHUNKS),
            sem(CHUNKS),
            sem(CHUNKS),
            sem(CHUNKS),
            sem(CHUNKS),
            sem(CHUNKS),
            sem(CHUNKS),
            sem(4),
            sem(QUARTERS),
            sem(QUARTERS),
            sem(QUARTERS),
            sem(QUARTERS),
        ],
        compiler_params=pltpu.CompilerParams(
            collective_id=0, has_side_effects=True, vmem_limit_bytes=40 << 20
        ),
        name="step",
    )(activations, out_grads, error_fb, q_prev)


def finish_kernel(p, w, q_t, hi, lo, out, q_new):
    @pl.when(pl.program_id(0) == 0)
    def _():
        q_new[...] = q_t[...].T

    high, low = halves(w[...])
    approx = dot(p[...], jnp.concatenate([high, high], axis=0)) + dot(p[:, :RANK], low)
    out[...] = ((hi[...].astype(F32) - approx) + lo[...].astype(F32)).astype(BF)


def finish(p, w, q_t, hi, lo):
    tile = 1024
    fixed = lambda *dims: pl.BlockSpec(dims, lambda i: (0, 0))
    moving = lambda *dims: pl.BlockSpec(dims, lambda i: (i, 0))
    return pl.pallas_call(
        finish_kernel,
        out_shape=[jax.ShapeDtypeStruct((ROWS, COLS), BF), jax.ShapeDtypeStruct((COLS, RANK), F32)],
        grid=(ROWS // tile,),
        in_specs=[
            moving(tile, 2 * RANK), fixed(RANK, COLS), fixed(RANK, COLS), moving(tile, COLS), moving(tile, COLS)
        ],
        out_specs=[moving(tile, COLS), fixed(COLS, RANK)],
        compiler_params=pltpu.CompilerParams(vmem_limit_bytes=24 << 20),
        name="finish",
    )(p, w, q_t, hi, lo)


def per_device(activations, out_grads, error_fb, q_prev):
    operands = (activations[0], out_grads[0], error_fb[0], q_prev)
    held = [pltpu.with_memory_space_constraint(each, pltpu.HBM) for each in operands]
    hi, lo, p, w, q_t = step(*held)
    new_error, q_new = finish(p, w, q_t, hi, lo)
    return (new_error[None], q_new)


def solution(mesh):
    placed = (P("dp", None, None), P("dp", None, "mp"), P("dp", None, "mp"), P("mp", None))
    return jax.shard_map(
        per_device,
        mesh=mesh,
        in_specs=placed,
        out_specs=(P("dp", None, "mp"), P("mp", None)),
        check_vma=False,
    )
```

```python
import jax
import jax.numpy as jnp
from jax import lax
from jax.experimental import pallas as pl
from jax.experimental.pallas import tpu as pltpu
from jax.sharding import PartitionSpec as P

MESH = pl.DeviceIdType.MESH
NX, NY, NZ = 4, 4, 8
TOK, ROWS, COLS, RANK = 1024, 4096, 512, 128
CHUNKS = 4
CHUNK = ROWS // CHUNKS
SUB = CHUNK // (4 * NX * NY)
MERGE = 512
BLOCK, GROUP = 32, 16
QUARTERS = COLS // RANK
BF, F32 = jnp.bfloat16, jnp.float32
HIGHEST = lax.Precision.HIGHEST
FIRST = (((0,), (0,)), ((), ()))


def position():
    dp, mp = lax.axis_index("dp"), lax.axis_index("mp")
    return lax.rem(mp, NX), mp // NX, dp // 2, lax.rem(dp, 2)


def device(x, y, z, c):
    return (z * 2 + c, y * NX + x)


def turn(own, d, n):
    return lax.rem(own + d, n)


def remote(src, dst, send, recv, where):
    return pltpu.make_async_remote_copy(
        src_ref=src, dst_ref=dst, send_sem=send, recv_sem=recv, device_id=where, device_id_type=MESH
    )


def drain(like, sem):
    pltpu.make_async_copy(like, like, sem).wait()


def loop(first, last, body):
    def step(k, carry):
        body(k)
        return carry

    lax.fori_loop(first, last, step, 0)


def halves(value):
    high = value.astype(BF)
    return high, (value - high.astype(F32)).astype(BF)


def dot(a, b, dims=(((1,), (0,)), ((), ()))):
    return lax.dot_general(a, b, dims, preferred_element_type=F32)


def eliminate(m, b):
    at = b * BLOCK
    row = lax.broadcasted_iota(jnp.int32, (BLOCK, RANK), 0)
    sides = [m[at : at + BLOCK, :RANK], m[at : at + BLOCK, RANK:]]
    for start in range(0, BLOCK, GROUP):
        columns = [
            jnp.broadcast_to(sides[0][:, at + j : at + j + 1], (BLOCK, RANK)) for j in range(start, start + GROUP)
        ]
        for t in range(GROUP):
            j = start + t
            scale = lax.rsqrt(columns[t][j : j + 1, :])
            factor = jnp.where(row > j, columns[t] * scale, 0.0)
            for other in range(t + 1, GROUP):
                columns[other] = columns[other] - factor * factor[start + other : start + other + 1, :]
            for i in range(2):
                pivot = sides[i][j : j + 1, :] * scale
                sides[i] = jnp.where(row == j, pivot, sides[i] - factor * pivot)
    block = jnp.concatenate(sides, axis=1)
    m[at : at + BLOCK, :] = block
    if at + BLOCK < RANK:
        update = lax.dot_general(sides[0], block, FIRST, precision=HIGHEST, preferred_element_type=F32)
        m[at + BLOCK :, :] -= update[at + BLOCK :, :]


def step_kernel(
    a, g, e, q,
    hi, lo, both, w_out, q_out,
    abuf, ebuf, gbuf, qbuf, tcat, qcat, p, h, r0, r1, u, r2, zs_buf, full,
    acc, sq, cross, m, s, s0, hs, s1, sall,
    asem, esem, gsem, qsem, send, got0, got1, got2, got3, got4, bak2, bak1, bak0,
    ssend, sgot0, sgot1, sbak1, sbak0,
):
    x, y, z, c = position()
    partner = device(x, y, z, 1 - c)
    xs = [device(turn(x, d, NX), y, z, c) for d in range(1, NX)]
    ys = [device(x, turn(y, d, NY), z, c) for d in range(1, NY)]
    zs = [device(x, y, turn(z, d, NZ), c) for d in range(1, NZ)]
    rows = lambda k: pl.ds(pl.multiple_of(k * CHUNK, CHUNK), CHUNK)

    barrier = pltpu.get_barrier_semaphore()
    for peer in zs + xs + ys + [partner]:
        pl.semaphore_signal(barrier, inc=1, device_id=peer, device_id_type=MESH)

    def load_a(k):
        return pltpu.make_async_copy(a.at[:, rows(k)], abuf.at[:, rows(k)], asem.at[k])

    def load_e(k):
        return pltpu.make_async_copy(e.at[rows(k)], ebuf.at[rows(k)], esem.at[k])

    load_q = pltpu.make_async_copy(q, qbuf, qsem)
    load_g = pltpu.make_async_copy(g, gbuf, gsem)
    load_q.start()
    load_g.start()

    def load(k):
        load_a(k).start()
        load_e(k).start()

    loop(0, CHUNKS, load)
    acc[...] = jnp.zeros_like(acc)
    sq[...] = jnp.zeros_like(sq)
    cross[...] = jnp.zeros_like(cross)
    load_q.wait()
    q_high, q_low = halves(qbuf[...])
    qcat[:, :RANK] = q_high
    qcat[:, RANK:] = q_low
    load_g.wait()
    wide = dot(gbuf[...], qcat[...])
    t_high, t_low = halves(wide[:, :RANK] + wide[:, RANK:])
    tcat[:, :RANK] = t_high
    tcat[:, RANK:] = t_low

    def left(k):
        load_a(k).wait()
        load_e(k).wait()
        wide = dot(abuf[:, rows(k)], tcat[...], FIRST) + dot(ebuf[rows(k)], qcat[...])
        p[k] = (wide[:, :RANK] + wide[:, RANK:]).reshape(2, 2, NX, NY, SUB, RANK)

    def merge(n):
        part = pl.ds(pl.multiple_of(n * MERGE, MERGE), MERGE)
        high, low = halves(dot(abuf[:, part], gbuf[...], FIRST) + ebuf[part].astype(F32))
        hi[part] = high
        lo[part] = low

    def pair(k):
        remote(p.at[k, 1 - c], r0.at[k], send.at[0], got0.at[k], partner).start()

    def first(k):
        drain(r0.at[k], got0.at[k])
        h[k] = p[k, c] + r0[k]
        for d in range(1, NX):
            remote(h.at[k, 0, turn(x, d, NX)], r1.at[k, 0, d - 1], send.at[1], got1.at[k], xs[d - 1]).start()
            remote(h.at[k, 1, turn(y, d, NY)], r1.at[k, 1, d - 1], send.at[1], got1.at[k], ys[d - 1]).start()

    def second(k):
        drain(r1.at[k], got1.at[k])
        for part, own in ((0, x), (1, y)):
            u[k, part] = h[k, part, own] + r1[k, part, 0] + r1[k, part, 1] + r1[k, part, 2]
        for d in range(1, NX):
            remote(u.at[k, 0, turn(y, d, NY)], r2.at[k, 0, d - 1], send.at[2], got2.at[k], ys[d - 1]).start()
            remote(u.at[k, 1, turn(x, d, NX)], r2.at[k, 1, d - 1], send.at[2], got2.at[k], xs[d - 1]).start()

    def third(k):
        drain(r2.at[k], got2.at[k])
        for part, own in ((0, y), (1, x)):
            zs_buf[k, z, part] = u[k, part, own] + r2[k, part, 0] + r2[k, part, 1] + r2[k, part, 2]
        for d in (1, 2, NZ - 2, NZ - 1):
            remote(zs_buf.at[k, z], zs_buf.at[k, z], send.at[3], got3.at[k], zs[d - 1]).start()

    def onward(k):
        drain(zs_buf.at[k, pl.ds(0, 4)], got3.at[k])
        for part, way in ((0, 1), (1, NZ - 1)):
            origin = turn(z, NZ - 2 if way == 1 else 2, NZ)
            whole, half = zs_buf.at[k, origin], zs_buf.at[k, origin, part]
            remote(whole, whole, send.at[7], got4.at[k], zs[way - 1]).start()
            remote(half, half, send.at[7], got4.at[k], zs[(2 * way) % NZ - 1]).start()

    def second_back(k):
        drain(zs_buf.at[k, pl.ds(0, 3)], got4.at[k])
        total = zs_buf[k, 0]
        for other in range(1, NZ):
            total = total + zs_buf[k, other]
        full[k, c, 0, x, y] = total[0]
        full[k, c, 1, y, x] = total[1]
        for d in range(1, NX):
            one, two = full.at[k, c, 0, x, y], full.at[k, c, 1, y, x]
            remote(one, one, send.at[4], bak2.at[k], ys[d - 1]).start()
            remote(two, two, send.at[4], bak2.at[k], xs[d - 1]).start()

    def first_back(k):
        drain(r2.at[k], bak2.at[k])
        for d in range(1, NX):
            one, two = full.at[k, c, 0, x], full.at[k, c, 1, y]
            remote(one, one, send.at[5], bak1.at[k], xs[d - 1]).start()
            remote(two, two, send.at[5], bak1.at[k], ys[d - 1]).start()

    def pair_back(k):
        drain(r1.at[k], bak1.at[k])
        remote(full.at[k, c], full.at[k, c], send.at[6], bak0.at[k], partner).start()

    def use(k, half):
        block = full[k, half].reshape(CHUNK // 2, RANK)
        part = pl.ds(pl.multiple_of(k * CHUNK + half * (CHUNK // 2), CHUNK // 2), CHUNK // 2)
        high, low = halves(block)
        rest = ((block - high.astype(F32)) - low.astype(F32)).astype(BF)
        both[part, :RANK] = high
        both[part, RANK:] = low
        wide = both[part]
        acc[...] += dot(wide, hi[part], FIRST)
        acc[:RANK] += dot(high, lo[part], FIRST)
        sq[...] += dot(wide, wide, FIRST)
        cross[...] += dot(high, rest, FIRST)

    def use_own(k):
        use(k, c)

    def use_other(k):
        drain(r0.at[k], bak0.at[k])
        use(k, 1 - c)

    early = 3
    loop(0, early, left)
    pl.semaphore_wait(barrier, 1 + len(xs) + len(ys) + len(zs))
    loop(0, early, pair)

    def late(k):
        left(k)
        pair(k)

    loop(early, CHUNKS, late)
    ahead = 3
    loop(0, ahead, first)
    stages = (
        (second, 3, 0, CHUNKS), (first, 0, ahead, CHUNKS), (third, 5, 0, CHUNKS), (onward, 8, 0, CHUNKS),
        (second_back, 10, 0, CHUNKS), (first_back, 12, 0, CHUNKS), (pair_back, 15, 0, CHUNKS),
        (merge, 0, 0, ROWS // MERGE), (use_own, 15, 0, CHUNKS), (use_other, 16, 0, CHUNKS),
    )

    def slot(t):
        for stage, lag, start, stop in stages:
            @pl.when((t >= lag + start) & (t < lag + stop))
            def _():
                stage(t - lag)

    loop(0, stages[-1][1] + CHUNKS, slot)

    own = acc[:RANK] + acc[RANK:]
    for n in range(QUARTERS):
        s[n] = own[:, n * RANK : (n + 1) * RANK].reshape(2, NZ, 8, RANK)
        remote(s.at[n, 1 - c], s0.at[n], ssend.at[0], sgot0.at[n], partner).start()
    mixed = sq[:RANK, RANK:] + cross[...]
    m[:, :RANK] = sq[:RANK, :RANK] + (sq[RANK:, RANK:] + (mixed + mixed.T))
    diagonal = lax.broadcasted_iota(jnp.int32, (RANK, RANK), 0) == lax.broadcasted_iota(jnp.int32, (RANK, RANK), 1)
    m[:, RANK:] = diagonal.astype(F32)

    def spread(n):
        drain(s0.at[n], sgot0.at[n])
        hs[n] = s[n, c] + s0[n]
        for d in range(1, NZ):
            remote(hs.at[n, turn(z, d, NZ)], s1.at[n, d - 1], ssend.at[1], sgot1.at[n], zs[d - 1]).start()

    def gather(n):
        drain(s1.at[n], sgot1.at[n])
        total = hs[n, z]
        for d in range(NZ - 1):
            total = total + s1[n, d]
        sall[n, c, z] = total
        piece = sall.at[n, c, z]
        for d in range(1, NZ):
            remote(piece, piece, ssend.at[2], sbak1.at[n], zs[d - 1]).start()

    def share(n):
        drain(s1.at[n], sbak1.at[n])
        remote(sall.at[n, c], sall.at[n, c], ssend.at[3], sbak0.at[n], partner).start()

    def factors(ns):
        for n in ns:
            drain(s0.at[n], sbak0.at[n])
        scaled = jnp.concatenate([sall[n].reshape(RANK, RANK) for n in ns], axis=1) * (1.0 / (2 * NZ))
        q_new = jnp.dot(m[:, RANK:], scaled, precision=HIGHEST, preferred_element_type=F32)
        columns = slice(ns[0] * RANK, (ns[-1] + 1) * RANK)
        q_out[:, columns] = q_new
        w_out[:, columns] = lax.dot_general(m[:, RANK:], q_new, FIRST, precision=HIGHEST, preferred_element_type=F32)

    eliminate(m, 0)
    loop(0, QUARTERS, spread)
    eliminate(m, 1)
    eliminate(m, 2)
    eliminate(m, 3)
    loop(0, QUARTERS, gather)
    loop(0, QUARTERS, share)
    factors((0, 1))
    factors((2, 3))

    drain(r0, send.at[0])
    drain(r1, send.at[1])
    drain(r2, send.at[2])
    drain(zs_buf.at[:, pl.ds(0, 4)], send.at[3])
    drain(zs_buf.at[:, pl.ds(0, 3)], send.at[7])
    drain(r2, send.at[4])
    drain(r1, send.at[5])
    drain(r0, send.at[6])
    drain(s0, ssend.at[0])
    drain(s1, ssend.at[1])
    drain(s1, ssend.at[2])
    drain(s0, ssend.at[3])


def step(activations, out_grads, error_fb, q_prev):
    far = pl.BlockSpec(memory_space=pltpu.HBM)
    near = pl.BlockSpec(memory_space=pltpu.VMEM)
    vm = lambda *dims: pltpu.VMEM(dims, F32)
    bf = lambda *dims: pltpu.VMEM(dims, BF)
    sem = lambda *dims: pltpu.SemaphoreType.DMA(dims)
    return pl.pallas_call(
        step_kernel,
        out_shape=[
            jax.ShapeDtypeStruct((ROWS, COLS), BF),
            jax.ShapeDtypeStruct((ROWS, COLS), BF),
            jax.ShapeDtypeStruct((ROWS, 2 * RANK), BF),
            jax.ShapeDtypeStruct((RANK, COLS), F32),
            jax.ShapeDtypeStruct((RANK, COLS), F32),
        ],
        in_specs=[far] * 4,
        out_specs=[near] * 5,
        scratch_shapes=[
            bf(TOK, ROWS),
            bf(ROWS, COLS),
            bf(TOK, COLS),
            vm(COLS, RANK),
            bf(TOK, 2 * RANK),
            bf(COLS, 2 * RANK),
            vm(CHUNKS, 2, 2, NX, NY, SUB, RANK),
            vm(CHUNKS, 2, NX, NY, SUB, RANK),
            vm(CHUNKS, 2, NX, NY, SUB, RANK),
            vm(CHUNKS, 2, NX - 1, NY, SUB, RANK),
            vm(CHUNKS, 2, NY, SUB, RANK),
            vm(CHUNKS, 2, NY - 1, SUB, RANK),
            vm(CHUNKS, NZ, 2, SUB, RANK),
            vm(CHUNKS, 2, 2, NX, NY, SUB, RANK),
            vm(2 * RANK, COLS),
            vm(2 * RANK, 2 * RANK),
            vm(RANK, RANK),
            vm(RANK, 2 * RANK),
            vm(QUARTERS, 2, NZ, 8, RANK),
            vm(QUARTERS, NZ, 8, RANK),
            vm(QUARTERS, NZ, 8, RANK),
            vm(QUARTERS, NZ - 1, 8, RANK),
            vm(QUARTERS, 2, NZ, 8, RANK),
            sem(CHUNKS),
            sem(CHUNKS),
            sem(),
            sem(),
            sem(8),
            sem(CHUNKS),
            sem(CHUNKS),
            sem(CHUNKS),
            sem(CHUNKS),
            sem(CHUNKS),
            sem(CHUNKS),
            sem(CHUNKS),
            sem(CHUNKS),
            sem(4),
            sem(QUARTERS),
            sem(QUARTERS),
            sem(QUARTERS),
            sem(QUARTERS),
        ],
        compiler_params=pltpu.CompilerParams(
            collective_id=0, has_side_effects=True, vmem_limit_bytes=40 << 20
        ),
        name="step",
    )(activations, out_grads, error_fb, q_prev)


def finish_kernel(p, w, q_t, hi, lo, out, q_new):
    @pl.when(pl.program_id(0) == 0)
    def _():
        q_new[...] = q_t[...].T

    high, low = halves(w[...])
    approx = dot(p[...], jnp.concatenate([high, high], axis=0)) + dot(p[:, :RANK], low)
    out[...] = ((hi[...].astype(F32) - approx) + lo[...].astype(F32)).astype(BF)


def finish(p, w, q_t, hi, lo):
    tile = 1024
    fixed = lambda *dims: pl.BlockSpec(dims, lambda i: (0, 0))
    moving = lambda *dims: pl.BlockSpec(dims, lambda i: (i, 0))
    return pl.pallas_call(
        finish_kernel,
        out_shape=[jax.ShapeDtypeStruct((ROWS, COLS), BF), jax.ShapeDtypeStruct((COLS, RANK), F32)],
        grid=(ROWS // tile,),
        in_specs=[
            moving(tile, 2 * RANK), fixed(RANK, COLS), fixed(RANK, COLS), moving(tile, COLS), moving(tile, COLS)
        ],
        out_specs=[moving(tile, COLS), fixed(COLS, RANK)],
        compiler_params=pltpu.CompilerParams(vmem_limit_bytes=24 << 20),
        name="finish",
    )(p, w, q_t, hi, lo)


def per_device(activations, out_grads, error_fb, q_prev):
    operands = (activations[0], out_grads[0], error_fb[0], q_prev)
    held = [pltpu.with_memory_space_constraint(each, pltpu.HBM) for each in operands]
    hi, lo, p, w, q_t = step(*held)
    new_error, q_new = finish(p, w, q_t, hi, lo)
    return (new_error[None], q_new)


def solution(mesh):
    placed = (P("dp", None, None), P("dp", None, "mp"), P("dp", None, "mp"), P("mp", None))
    return jax.shard_map(
        per_device,
        mesh=mesh,
        in_specs=placed,
        out_specs=(P("dp", None, "mp"), P("mp", None)),
        check_vma=False,
    )
```

```python
import jax
import jax.numpy as jnp
from jax import lax
from jax.experimental import pallas as pl
from jax.experimental.pallas import tpu as pltpu
from jax.sharding import PartitionSpec as P

MESH = pl.DeviceIdType.MESH
NX, NY, NZ = 4, 4, 8
TOK, ROWS, COLS, RANK = 1024, 4096, 512, 128
CHUNKS = 4
CHUNK = ROWS // CHUNKS
SUB = CHUNK // (4 * NX * NY)
MERGE = 512
TILE = 512
BLOCK, GROUP = 32, 16
QUARTERS = COLS // RANK
BF, F32 = jnp.bfloat16, jnp.float32
HIGHEST = lax.Precision.HIGHEST
FIRST = (((0,), (0,)), ((), ()))


def position():
    dp, mp = lax.axis_index("dp"), lax.axis_index("mp")
    return lax.rem(mp, NX), mp // NX, dp // 2, lax.rem(dp, 2)


def device(x, y, z, c):
    return (z * 2 + c, y * NX + x)


def turn(own, d, n):
    return lax.rem(own + d, n)


def remote(src, dst, send, recv, where):
    return pltpu.make_async_remote_copy(
        src_ref=src, dst_ref=dst, send_sem=send, recv_sem=recv, device_id=where, device_id_type=MESH
    )


def drain(like, sem):
    pltpu.make_async_copy(like, like, sem).wait()


def loop(first, last, body):
    def step(k, carry):
        body(k)
        return carry

    lax.fori_loop(first, last, step, 0)


def halves(value):
    high = value.astype(BF)
    return high, (value - high.astype(F32)).astype(BF)


def dot(a, b, dims=(((1,), (0,)), ((), ()))):
    return lax.dot_general(a, b, dims, preferred_element_type=F32)


def eliminate(m, b):
    at = b * BLOCK
    row = lax.broadcasted_iota(jnp.int32, (BLOCK, RANK), 0)
    sides = [m[at : at + BLOCK, :RANK], m[at : at + BLOCK, RANK:]]
    for start in range(0, BLOCK, GROUP):
        columns = [
            jnp.broadcast_to(sides[0][:, at + j : at + j + 1], (BLOCK, RANK)) for j in range(start, start + GROUP)
        ]
        for t in range(GROUP):
            j = start + t
            scale = lax.rsqrt(columns[t][j : j + 1, :])
            factor = jnp.where(row > j, columns[t] * scale, 0.0)
            for other in range(t + 1, GROUP):
                columns[other] = columns[other] - factor * factor[start + other : start + other + 1, :]
            for i in range(2):
                pivot = sides[i][j : j + 1, :] * scale
                sides[i] = jnp.where(row == j, pivot, sides[i] - factor * pivot)
    block = jnp.concatenate(sides, axis=1)
    m[at : at + BLOCK, :] = block
    if at + BLOCK < RANK:
        update = lax.dot_general(sides[0], block, FIRST, precision=HIGHEST, preferred_element_type=F32)
        m[at + BLOCK :, :] -= update[at + BLOCK :, :]


def step_kernel(
    a, g, e, q,
    hi, lo, both, w_out, q_out,
    abuf, ebuf, gbuf, qbuf, tcat, qcat, p, h, r0, r1, u, r2, zs_buf, full,
    acc, sq, cross, m, s, s0, hs, s1, sall,
    asem, esem, gsem, qsem, send, got0, got1, got2, got3, got4, bak2, bak1, bak0,
    ssend, sgot0, sgot1, sbak1, sbak0,
):
    x, y, z, c = position()
    partner = device(x, y, z, 1 - c)
    xs = [device(turn(x, d, NX), y, z, c) for d in range(1, NX)]
    ys = [device(x, turn(y, d, NY), z, c) for d in range(1, NY)]
    zs = [device(x, y, turn(z, d, NZ), c) for d in range(1, NZ)]
    rows = lambda k: pl.ds(pl.multiple_of(k * CHUNK, CHUNK), CHUNK)

    barrier = pltpu.get_barrier_semaphore()
    for peer in zs + xs + ys + [partner]:
        pl.semaphore_signal(barrier, inc=1, device_id=peer, device_id_type=MESH)

    def load_a(k):
        return pltpu.make_async_copy(a.at[:, rows(k)], abuf.at[:, rows(k)], asem.at[k])

    def load_e(k):
        return pltpu.make_async_copy(e.at[rows(k)], ebuf.at[rows(k)], esem.at[k])

    load_q = pltpu.make_async_copy(q, qbuf, qsem)
    load_g = pltpu.make_async_copy(g, gbuf, gsem)
    load_q.start()
    load_g.start()

    def load(k):
        load_a(k).start()
        load_e(k).start()

    loop(0, CHUNKS, load)
    acc[...] = jnp.zeros_like(acc)
    sq[...] = jnp.zeros_like(sq)
    cross[...] = jnp.zeros_like(cross)
    load_q.wait()
    q_high, q_low = halves(qbuf[...])
    qcat[:, :RANK] = q_high
    qcat[:, RANK:] = q_low
    load_g.wait()
    wide = dot(gbuf[...], qcat[...])
    t_high, t_low = halves(wide[:, :RANK] + wide[:, RANK:])
    tcat[:, :RANK] = t_high
    tcat[:, RANK:] = t_low

    def left(k):
        load_a(k).wait()
        load_e(k).wait()
        wide = dot(abuf[:, rows(k)], tcat[...], FIRST) + dot(ebuf[rows(k)], qcat[...])
        p[k] = (wide[:, :RANK] + wide[:, RANK:]).reshape(2, 2, NX, NY, SUB, RANK)

    def merge(n):
        part = pl.ds(pl.multiple_of(n * MERGE, MERGE), MERGE)
        high, low = halves(dot(abuf[:, part], gbuf[...], FIRST) + ebuf[part].astype(F32))
        hi[part] = high
        lo[part] = low

    def pair(k):
        remote(p.at[k, 1 - c], r0.at[k], send.at[0], got0.at[k], partner).start()

    def first(k):
        drain(r0.at[k], got0.at[k])
        h[k] = p[k, c] + r0[k]
        for d in range(1, NX):
            remote(h.at[k, 0, turn(x, d, NX)], r1.at[k, 0, d - 1], send.at[1], got1.at[k], xs[d - 1]).start()
            remote(h.at[k, 1, turn(y, d, NY)], r1.at[k, 1, d - 1], send.at[1], got1.at[k], ys[d - 1]).start()

    def second(k):
        drain(r1.at[k], got1.at[k])
        for part, own in ((0, x), (1, y)):
            u[k, part] = h[k, part, own] + r1[k, part, 0] + r1[k, part, 1] + r1[k, part, 2]
        for d in range(1, NX):
            remote(u.at[k, 0, turn(y, d, NY)], r2.at[k, 0, d - 1], send.at[2], got2.at[k], ys[d - 1]).start()
            remote(u.at[k, 1, turn(x, d, NX)], r2.at[k, 1, d - 1], send.at[2], got2.at[k], xs[d - 1]).start()

    def third(k):
        drain(r2.at[k], got2.at[k])
        for part, own in ((0, y), (1, x)):
            zs_buf[k, z, part] = u[k, part, own] + r2[k, part, 0] + r2[k, part, 1] + r2[k, part, 2]
        for d in (1, 2, NZ - 2, NZ - 1):
            remote(zs_buf.at[k, z], zs_buf.at[k, z], send.at[3], got3.at[k], zs[d - 1]).start()

    def onward(k):
        drain(zs_buf.at[k, pl.ds(0, 4)], got3.at[k])
        for part, way in ((0, 1), (1, NZ - 1)):
            origin = turn(z, NZ - 2 if way == 1 else 2, NZ)
            whole, half = zs_buf.at[k, origin], zs_buf.at[k, origin, part]
            remote(whole, whole, send.at[7], got4.at[k], zs[way - 1]).start()
            remote(half, half, send.at[7], got4.at[k], zs[(2 * way) % NZ - 1]).start()

    def second_back(k):
        drain(zs_buf.at[k, pl.ds(0, 3)], got4.at[k])
        total = zs_buf[k, 0]
        for other in range(1, NZ):
            total = total + zs_buf[k, other]
        full[k, c, 0, x, y] = total[0]
        full[k, c, 1, y, x] = total[1]
        for d in range(1, NX):
            one, two = full.at[k, c, 0, x, y], full.at[k, c, 1, y, x]
            remote(one, one, send.at[4], bak2.at[k], ys[d - 1]).start()
            remote(two, two, send.at[4], bak2.at[k], xs[d - 1]).start()

    def first_back(k):
        drain(r2.at[k], bak2.at[k])
        for d in range(1, NX):
            one, two = full.at[k, c, 0, x], full.at[k, c, 1, y]
            remote(one, one, send.at[5], bak1.at[k], xs[d - 1]).start()
            remote(two, two, send.at[5], bak1.at[k], ys[d - 1]).start()

    def pair_back(k):
        drain(r1.at[k], bak1.at[k])
        remote(full.at[k, c], full.at[k, c], send.at[6], bak0.at[k], partner).start()

    def use(k, half):
        block = full[k, half].reshape(CHUNK // 2, RANK)
        part = pl.ds(pl.multiple_of(k * CHUNK + half * (CHUNK // 2), CHUNK // 2), CHUNK // 2)
        high, low = halves(block)
        rest = ((block - high.astype(F32)) - low.astype(F32)).astype(BF)
        both[part, :RANK] = high
        both[part, RANK:] = low
        wide = both[part]
        acc[...] += dot(wide, hi[part], FIRST)
        acc[:RANK] += dot(high, lo[part], FIRST)
        sq[...] += dot(wide, wide, FIRST)
        cross[...] += dot(high, rest, FIRST)

    def use_own(k):
        use(k, c)

    def use_other(k):
        drain(r0.at[k], bak0.at[k])
        use(k, 1 - c)

    early = 3
    loop(0, early, left)
    pl.semaphore_wait(barrier, 1 + len(xs) + len(ys) + len(zs))
    loop(0, early, pair)

    def late(k):
        left(k)
        pair(k)

    loop(early, CHUNKS, late)
    ahead = 3
    loop(0, ahead, first)
    stages = (
        (second, 3, 0, CHUNKS), (first, 0, ahead, CHUNKS), (third, 5, 0, CHUNKS), (onward, 8, 0, CHUNKS),
        (second_back, 10, 0, CHUNKS), (first_back, 12, 0, CHUNKS), (pair_back, 15, 0, CHUNKS),
        (merge, 0, 0, ROWS // MERGE), (use_own, 15, 0, CHUNKS), (use_other, 16, 0, CHUNKS),
    )

    def slot(t):
        for stage, lag, start, stop in stages:
            @pl.when((t >= lag + start) & (t < lag + stop))
            def _():
                stage(t - lag)

    loop(0, stages[-1][1] + CHUNKS, slot)

    own = acc[:RANK] + acc[RANK:]
    for n in range(QUARTERS):
        s[n] = own[:, n * RANK : (n + 1) * RANK].reshape(2, NZ, 8, RANK)
        remote(s.at[n, 1 - c], s0.at[n], ssend.at[0], sgot0.at[n], partner).start()
    mixed = sq[:RANK, RANK:] + cross[...]
    m[:, :RANK] = sq[:RANK, :RANK] + (sq[RANK:, RANK:] + (mixed + mixed.T))
    diagonal = lax.broadcasted_iota(jnp.int32, (RANK, RANK), 0) == lax.broadcasted_iota(jnp.int32, (RANK, RANK), 1)
    m[:, RANK:] = diagonal.astype(F32)

    def spread(n):
        drain(s0.at[n], sgot0.at[n])
        hs[n] = s[n, c] + s0[n]
        for d in range(1, NZ):
            remote(hs.at[n, turn(z, d, NZ)], s1.at[n, d - 1], ssend.at[1], sgot1.at[n], zs[d - 1]).start()

    def gather(n):
        drain(s1.at[n], sgot1.at[n])
        total = hs[n, z]
        for d in range(NZ - 1):
            total = total + s1[n, d]
        sall[n, c, z] = total
        piece = sall.at[n, c, z]
        for d in range(1, NZ):
            remote(piece, piece, ssend.at[2], sbak1.at[n], zs[d - 1]).start()

    def share(n):
        drain(s1.at[n], sbak1.at[n])
        remote(sall.at[n, c], sall.at[n, c], ssend.at[3], sbak0.at[n], partner).start()

    def factors(ns):
        for n in ns:
            drain(s0.at[n], sbak0.at[n])
        scaled = jnp.concatenate([sall[n].reshape(RANK, RANK) for n in ns], axis=1) * (1.0 / (2 * NZ))
        q_new = jnp.dot(m[:, RANK:], scaled, precision=HIGHEST, preferred_element_type=F32)
        columns = slice(ns[0] * RANK, (ns[-1] + 1) * RANK)
        q_out[:, columns] = q_new
        w_out[:, columns] = lax.dot_general(m[:, RANK:], q_new, FIRST, precision=HIGHEST, preferred_element_type=F32)

    eliminate(m, 0)
    loop(0, QUARTERS, spread)
    eliminate(m, 1)
    eliminate(m, 2)
    eliminate(m, 3)
    loop(0, QUARTERS, gather)
    loop(0, QUARTERS, share)
    factors((0, 1))
    factors((2, 3))

    drain(r0, send.at[0])
    drain(r1, send.at[1])
    drain(r2, send.at[2])
    drain(zs_buf.at[:, pl.ds(0, 4)], send.at[3])
    drain(zs_buf.at[:, pl.ds(0, 3)], send.at[7])
    drain(r2, send.at[4])
    drain(r1, send.at[5])
    drain(r0, send.at[6])
    drain(s0, ssend.at[0])
    drain(s1, ssend.at[1])
    drain(s1, ssend.at[2])
    drain(s0, ssend.at[3])


def step(activations, out_grads, error_fb, q_prev):
    far = pl.BlockSpec(memory_space=pltpu.HBM)
    near = pl.BlockSpec(memory_space=pltpu.VMEM)
    vm = lambda *dims: pltpu.VMEM(dims, F32)
    bf = lambda *dims: pltpu.VMEM(dims, BF)
    sem = lambda *dims: pltpu.SemaphoreType.DMA(dims)
    return pl.pallas_call(
        step_kernel,
        out_shape=[
            jax.ShapeDtypeStruct((ROWS, COLS), BF),
            jax.ShapeDtypeStruct((ROWS, COLS), BF),
            jax.ShapeDtypeStruct((ROWS, 2 * RANK), BF),
            jax.ShapeDtypeStruct((RANK, COLS), F32),
            jax.ShapeDtypeStruct((RANK, COLS), F32),
        ],
        in_specs=[far] * 4,
        out_specs=[near] * 5,
        scratch_shapes=[
            bf(TOK, ROWS),
            bf(ROWS, COLS),
            bf(TOK, COLS),
            vm(COLS, RANK),
            bf(TOK, 2 * RANK),
            bf(COLS, 2 * RANK),
            vm(CHUNKS, 2, 2, NX, NY, SUB, RANK),
            vm(CHUNKS, 2, NX, NY, SUB, RANK),
            vm(CHUNKS, 2, NX, NY, SUB, RANK),
            vm(CHUNKS, 2, NX - 1, NY, SUB, RANK),
            vm(CHUNKS, 2, NY, SUB, RANK),
            vm(CHUNKS, 2, NY - 1, SUB, RANK),
            vm(CHUNKS, NZ, 2, SUB, RANK),
            vm(CHUNKS, 2, 2, NX, NY, SUB, RANK),
            vm(2 * RANK, COLS),
            vm(2 * RANK, 2 * RANK),
            vm(RANK, RANK),
            vm(RANK, 2 * RANK),
            vm(QUARTERS, 2, NZ, 8, RANK),
            vm(QUARTERS, NZ, 8, RANK),
            vm(QUARTERS, NZ, 8, RANK),
            vm(QUARTERS, NZ - 1, 8, RANK),
            vm(QUARTERS, 2, NZ, 8, RANK),
            sem(CHUNKS),
            sem(CHUNKS),
            sem(),
            sem(),
            sem(8),
            sem(CHUNKS),
            sem(CHUNKS),
            sem(CHUNKS),
            sem(CHUNKS),
            sem(CHUNKS),
            sem(CHUNKS),
            sem(CHUNKS),
            sem(CHUNKS),
            sem(4),
            sem(QUARTERS),
            sem(QUARTERS),
            sem(QUARTERS),
            sem(QUARTERS),
        ],
        compiler_params=pltpu.CompilerParams(
            collective_id=0, has_side_effects=True, vmem_limit_bytes=40 << 20
        ),
        name="step",
    )(activations, out_grads, error_fb, q_prev)


def finish_kernel(p, w, q_t, hi, lo, out, q_new, weights, ready, sem):
    high, low = halves(w[...])
    weights[:RANK] = high
    weights[RANK : 2 * RANK] = high
    weights[2 * RANK :] = low

    def tile(k):
        part = slice(k * TILE, (k + 1) * TILE)
        approx = dot(p[part], weights[: 2 * RANK]) + dot(p[part, :RANK], weights[2 * RANK :])
        ready[part] = ((hi[part].astype(F32) - approx) + lo[part].astype(F32)).astype(BF)
        pltpu.make_async_copy(ready.at[part], out.at[part], sem).start()

    for k in range(ROWS // TILE):
        tile(k)
    q_new[...] = q_t[...].T
    pltpu.make_async_copy(ready, out, sem).wait()


def finish(p, w, q_t, hi, lo):
    near = pl.BlockSpec(memory_space=pltpu.VMEM)
    return pl.pallas_call(
        finish_kernel,
        out_shape=[jax.ShapeDtypeStruct((ROWS, COLS), BF), jax.ShapeDtypeStruct((COLS, RANK), F32)],
        in_specs=[near] * 5,
        out_specs=[pl.BlockSpec(memory_space=pltpu.HBM), near],
        scratch_shapes=[
            pltpu.VMEM((3 * RANK, COLS), BF), pltpu.VMEM((ROWS, COLS), BF), pltpu.SemaphoreType.DMA(())
        ],
        compiler_params=pltpu.CompilerParams(vmem_limit_bytes=24 << 20),
        name="finish",
    )(p, w, q_t, hi, lo)


def per_device(activations, out_grads, error_fb, q_prev):
    operands = (activations[0], out_grads[0], error_fb[0], q_prev)
    held = [pltpu.with_memory_space_constraint(each, pltpu.HBM) for each in operands]
    hi, lo, p, w, q_t = step(*held)
    new_error, q_new = finish(p, w, q_t, hi, lo)
    return (new_error[None], q_new)


def solution(mesh):
    placed = (P("dp", None, None), P("dp", None, "mp"), P("dp", None, "mp"), P("mp", None))
    return jax.shard_map(
        per_device,
        mesh=mesh,
        in_specs=placed,
        out_specs=(P("dp", None, "mp"), P("mp", None)),
        check_vma=False,
    )
```
